256 devices in a mesh: tests: 64 (over z, x, core), branches: 4 (over y).
Axes of the slice: x: 4, y: 4, z: 8, core: 2. Of those that a mesh axis runs over, the one named last changes fastest.
Arguments:
- select: float32 [1048576], P('tests'), may hold values from 1e-05 to 0.95
- tiles: float32 [16384, 128, 128], P(('tests', 'branches')), may hold values from 0.0001 to 0.9
- row_block: int32 [16384], P(('tests', 'branches')), may hold values from 0 to 127
- col_block: int32 [16384], P(('tests', 'branches')), may hold values from 0 to 2047, as said below
- counts: int32 [256], P(('tests', 'branches')), may hold values from 1 to 64, 10240 in all
- weights: float32 [1048576], P('branches'), may hold values from 1 to 16
Outputs:
- grad_tests: float32 [1048576], P('tests')
- tile_grads: float32 [16384, 128, 128], P(('tests', 'branches'))
- next_select: float32 [1048576], P('tests')
The draws below stay inside these ranges and needn't reach their ends.
Inputs may be any that keep to these rules, and one draw needn't show every extreme that they name: counts[d] is the number of device d's slots, from its first, that hold tiles. Call col_block[s] // 32 the share of slot s. Of the 64 slots of one device at most 2 have one share; in every index of branches one share holds exactly 2 slots of every device there.
All inputs are finite; a program needn't handle non-finite values.
Results may differ from the reference program's by a relative error of at most 0.0003.
Values sent between devices are 32-bit elements; how exact they have to be, the bound alone decides.
A program may use at most 64 MiB of HBM per device.

```python
import math
import jax
import jax.numpy as jnp
import numpy as np
from jax import lax

TILE = 128
CAP = 64
TB_DEV = 128
BB_DEV = 2048
STEPS = 2
TESTS = 1048576
BRANCHES = 1048576
SLOTS = 16384
FILLED = 10240
ROUTE = 2
N_TESTS = 64
N_BRANCHES = 4


def draw_col_block(key, part):
    key = jax.random.fold_in(key, 7)
    devices = N_TESTS * N_BRANCHES
    share = BB_DEV // N_TESTS
    seats = (N_TESTS - 1) * ROUTE
    rest = CAP - ROUTE
    full_owner = jax.random.randint(jax.random.fold_in(key, 1), (N_BRANCHES,), 0, N_TESTS).astype(jnp.int32)
    device_full = jnp.tile(full_owner, N_TESTS)
    scores = jax.random.randint(jax.random.fold_in(key, 2), (devices, seats), 0, 1 << 15).astype(jnp.int32)
    scores = scores * seats + jnp.arange(seats, dtype=jnp.int32)[None, :]
    order = jnp.argsort(scores, axis=1, stable=True)[:, :rest].astype(jnp.int32)
    other_rank = order // ROUTE
    others = other_rank + (other_rank >= device_full[:, None]).astype(jnp.int32)
    offset = jax.random.randint(jax.random.fold_in(key, 3), (devices,), 0, rest + 1).astype(jnp.int32)
    position = jnp.arange(CAP, dtype=jnp.int32)[None, :]
    in_group = (position >= offset[:, None]) & (position < offset[:, None] + ROUTE)
    index = jnp.where(position < offset[:, None], position, position - ROUTE)
    index = jnp.clip(index, 0, rest - 1).astype(jnp.int32)
    picked = jnp.take_along_axis(others, index, axis=1)
    owners = jnp.where(in_group, device_full[:, None], picked)
    inside = jax.random.randint(jax.random.fold_in(key, 4), (devices, CAP), 0, share).astype(jnp.int32)
    return (owners * share + inside).reshape(-1).astype(jnp.int32)


def plant(drawn, key, smallest, high):
    longest = drawn.shape.index(max(drawn.shape))
    spots = []
    for shift in (0, 1):
        where = [jax.random.randint(jax.random.fold_in(key, axis), (), 0, length) for axis, length in enumerate(drawn.shape)]
        where[longest] = (where[longest] + shift) % drawn.shape[longest]
        spots.append(tuple(where))
    return drawn.at[spots[0]].set(smallest).at[spots[1]].set(high)


def block_levels(key, extent, shards, low, top_value):
    factor_of, own = 1.0, jax.random.fold_in(key, 6)
    for dim, shards_of in shards:
        steps = jnp.exp(jax.random.uniform(jax.random.fold_in(own, dim), (shards_of,), jnp.float32, low / len(shards), top_value / len(shards)))
        factor_of = factor_of * jnp.repeat(steps, extent[dim] // shards_of).reshape([-1 if axis == dim else 1 for axis in range(len(extent))])
    return factor_of


def split_up(count, total, reach, slope):
    loads = [(1 << 20) // math.isqrt(rank ** slope) + 1 for rank in range(2, count + 1)]
    spare, holding = total - reach - (count - 1), [1] * (count - 1)
    while spare > 0:
        free = [i for i in range(count - 1) if holding[i] < reach]
        whole, budget = sum([loads[i] for i in free]), spare
        for i in free:
            more = min(reach - holding[i], max(1, budget * loads[i] // whole), spare)
            holding[i] = holding[i] + more
            spare = spare - more
    return np.array([reach] + holding)


def uneven_parts(stream_key, count, total, limit, lean):
    if count == 2:
        one = jax.random.randint(stream_key, (), max(1, total - limit), min(limit, total - 1) + 1)
        return jnp.stack([one, total - one])
    sizes = jnp.asarray(split_up(count, total, limit, lean), jnp.int32)
    pairs = (count - 1) // 2
    giver, taker = sizes[1:1 + 2 * pairs:2], sizes[2:2 + 2 * pairs:2]
    slack = jnp.minimum(giver - 1, limit - taker)
    moved = jax.random.randint(jax.random.fold_in(stream_key, 1), (pairs,), 0, 1 << 20) % (slack + 1)
    sizes = sizes.at[1:1 + 2 * pairs:2].set(giver - moved).at[2:2 + 2 * pairs:2].set(taker + moved)
    return sizes[jax.random.permutation(jax.random.fold_in(stream_key, 2), count)]


def setup_inputs(seed: int = 0) -> dict:
    seeds = jax.random.split(jax.random.key(seed), 7)
    select = jnp.clip(jnp.exp(math.log(0.95) - 11.461632 * jax.random.uniform(seeds[0], (TESTS,), jnp.float32) ** block_levels(seeds[0], (TESTS,), ((0, 64),), -0.2, 0.2)), 9.999999747378752e-06, 0.95)
    tiles = jnp.clip(jnp.exp(math.log(0.9) - 9.1049799 * jax.random.uniform(seeds[1], (SLOTS, TILE, TILE), jnp.float32) ** block_levels(seeds[1], (SLOTS, TILE, TILE), ((0, 256),), -0.2, 0.2)), 0.0001, 0.9)
    row_block = plant(jax.random.randint(seeds[2], (SLOTS,), 0, TB_DEV), jax.random.fold_in(seeds[2], 1), 0, TB_DEV - 1).astype(jnp.int32)
    col_block = draw_col_block(jax.random.fold_in(seeds[6], 71), 0)
    counts = uneven_parts(seeds[4], N_TESTS * N_BRANCHES, FILLED, CAP, 2).astype(jnp.int32)
    weights = jnp.clip(jnp.exp(math.log(16.0) - 2.7725887 * jax.random.uniform(seeds[5], (BRANCHES,), jnp.float32) ** block_levels(seeds[5], (BRANCHES,), ((0, 4),), -0.2, 0.2)), 1.0, 16.0)
    return dict(select=select, tiles=tiles, row_block=row_block, col_block=col_block, counts=counts, weights=weights)


ascent_rate = 0.0015
select_cap = 0.5


def device_layout(device, row_block, col_block, counts):
    start = device * CAP
    rows = lax.dynamic_slice_in_dim(row_block, start, CAP) + (device // N_BRANCHES) * TB_DEV
    columns = lax.dynamic_slice_in_dim(col_block, start, CAP) + (device % N_BRANCHES) * BB_DEV
    live = jnp.arange(CAP, dtype=jnp.int32) < counts[device]
    return start, rows.astype(jnp.int32), columns.astype(jnp.int32), live


def log_survival(current, tiles, row_block, col_block, counts):
    blocks = current.reshape(TB_DEV * N_TESTS, TILE)

    def visit(total, device):
        start, rows, columns, live = device_layout(device, row_block, col_block, counts)
        piece = lax.dynamic_slice_in_dim(tiles, start, CAP)
        picked = blocks[rows]
        logs = jnp.sum(jnp.log1p(-picked[:, :, None] * piece), axis=1)
        logs = jnp.where(live[:, None], logs, jnp.zeros_like(logs))
        return total.at[columns].add(logs), None

    zero = jnp.zeros((BB_DEV * N_BRANCHES, TILE), jnp.float32)
    total, _ = lax.scan(visit, zero, jnp.arange(N_TESTS * N_BRANCHES, dtype=jnp.int32))
    return total


def gradients(current, survival, tiles, row_block, col_block, counts, keep_tiles):
    blocks = current.reshape(TB_DEV * N_TESTS, TILE)

    def visit(total, device):
        start, rows, columns, live = device_layout(device, row_block, col_block, counts)
        piece = lax.dynamic_slice_in_dim(tiles, start, CAP)
        picked = blocks[rows]
        inverse = 1.0 / (1.0 - picked[:, :, None] * piece)
        scaled = survival[columns][:, None, :] * inverse
        terms = jnp.sum(scaled * piece, axis=2)
        terms = jnp.where(live[:, None], terms, jnp.zeros_like(terms))
        total = total.at[rows].add(terms)
        if keep_tiles:
            tile_part = scaled * picked[:, :, None]
            tile_part = jnp.where(live[:, None, None], tile_part, jnp.zeros_like(tile_part))
            return total, tile_part
        return total, None

    zero = jnp.zeros((TB_DEV * N_TESTS, TILE), jnp.float32)
    total, tile_parts = lax.scan(visit, zero, jnp.arange(N_TESTS * N_BRANCHES, dtype=jnp.int32))
    return total.reshape(-1), tile_parts


def reference(select, tiles, row_block, col_block, counts, weights):
    current = select
    weight_rows = weights.reshape(BB_DEV * N_BRANCHES, TILE)
    grad_tests = current
    tile_grads = tiles
    for step in range(STEPS):
        keep = step == STEPS - 1
        summed = log_survival(current, tiles, row_block, col_block, counts)
        survival = weight_rows * jnp.exp(summed)
        gradient, tile_parts = gradients(current, survival, tiles, row_block, col_block, counts, keep)
        if keep:
            grad_tests = gradient
            tile_grads = tile_parts.reshape(SLOTS, TILE, TILE)
        rate = ascent_rate * gradient
        current = current + (select_cap - current) * rate / (1.0 + rate)
    return grad_tests, tile_grads, current
```

```python
import functools

import jax
import jax.numpy as jnp
from jax import lax
from jax.experimental import pallas as pl
from jax.experimental.pallas import tpu as pltpu
from jax.sharding import PartitionSpec as P

MESH = pl.DeviceIdType.MESH
STEPS = 2
WIDTH = 128
GROUP = 8
CHAIN = 16
Z, X, C = 8, 4, 2

ascent_rate = 0.0015
select_cap = 0.5

exact = functools.partial(
    lax.dot_general,
    precision=lax.Precision.HIGHEST,
    preferred_element_type=jnp.float32,
)
ROWS = (((0,), (0,)), ((), ()))
PLAIN = (((1,), (0,)), ((), ()))


def iota(shape, axis):
    return lax.broadcasted_iota(jnp.int32, shape, axis)


def zigzag(k, size):
    half = (k + 1) // 2
    return size // 2 + half * (1 - 2 * (k % 2))


def ascend_kernel(
    n, share, slots, n_branches,
    select, rows, cols, counts, tiles_h, weights_h,
    grad_o, next_o, surv_o, cur_o,
    tiles_v, terms_v, meta_v, logs_v, surv_v, pick_v, route_v, hold_v, place_v, weights_v,
    a_send0, a_recv0, a_send1, a_recv1, b_send0, b_recv0, b_send1, b_recv1,
    g_send0, g_recv0, g_send1, g_recv1,
    tile_sem, local_sem, send_sem, recv_sem,
):
    t = lax.axis_index("tests")
    y = lax.axis_index("branches")
    z, x, c = t // (X * C), (t // C) % X, t % C
    groups = slots // GROUP

    def fetch(g):
        part = pl.ds(pl.multiple_of(g * GROUP, GROUP), GROUP)
        return pltpu.make_async_copy(tiles_h.at[part], tiles_v.at[part], tile_sem.at[g])

    for g in range(groups):
        fetch(g).start()
    own_weights = pltpu.make_async_copy(
        weights_h.at[pl.ds(pl.multiple_of(t * share, share), share)], weights_v, local_sem
    )
    own_weights.start()

    def ahead(i):
        dz, dx, dc = zigzag(i // (X * C), Z), zigzag((i // C) % X, X), 1 - i % C
        to = ((z + dz) % Z) * (X * C) + ((x + dx) % X) * C + (c + dc) % C
        back = ((z + Z - dz) % Z) * (X * C) + ((x + X - dx) % X) * C + (c + dc) % C
        return dz * (X * C) + dx * C + dc, to, back

    barrier = pltpu.get_barrier_semaphore()

    def greet(i, carry):
        _, to, _ = ahead(i)
        pl.semaphore_signal(barrier, inc=1, device_id=(to, y), device_id_type=MESH)
        return carry

    lax.fori_loop(0, n - 1, greet, 0)
    for d in range(1, n_branches):
        pl.semaphore_signal(
            barrier, inc=1, device_id=(t, (y + d) % n_branches), device_id_type=MESH
        )

    meta_v[...] = jnp.full_like(meta_v, -1)
    meta_v[0:1, 0:slots] = rows[...]
    meta_v[1:2, 0:slots] = cols[...]
    limit = counts[...]
    row_of, col_of = meta_v[0:1, :], meta_v[1:2, :]
    lane = iota((1, WIDTH), 1)
    live = lane < limit
    pick = (iota((WIDTH, WIDTH), 0) == row_of).astype(jnp.float32)
    pick_v[...] = pick
    owner, inside = col_of // share, col_of % share
    oz, ox, oc = owner // (X * C), (owner // C) % X, owner % C
    seat = ((oz + Z - z) % Z) * (X * C) + ((ox + X - x) % X) * C + (oc + C - c) % C
    seat = jnp.where(live, seat, n)
    takes = (iota((n, WIDTH), 0) == seat).astype(jnp.float32)
    earlier = (iota((WIDTH, WIDTH), 0) < iota((WIDTH, WIDTH), 1)).astype(jnp.float32)
    before = exact(takes, earlier, PLAIN)
    first = jnp.where(before < 0.5, takes, 0.0)
    second = takes - first
    route_v[0:n, :] = first
    route_v[n:2 * n, :] = second
    tag = (inside + 1).astype(jnp.float32)
    tag0 = jnp.sum(first * tag, axis=1, keepdims=True) - 1.0
    tag1 = jnp.sum(second * tag, axis=1, keepdims=True) - 1.0
    a_send0[:, 2, :] = jnp.where(iota((n, WIDTH), 1) < WIDTH // 2, tag0, tag1)

    logs_v[...] = jnp.zeros_like(logs_v)
    alive = iota((WIDTH, WIDTH), 0) < limit

    def send_all(src, dst, k, back):
        def one(i, carry):
            r, to, fro = ahead(i)
            pltpu.make_async_remote_copy(
                src_ref=src.at[r],
                dst_ref=dst.at[r],
                send_sem=send_sem.at[k],
                recv_sem=recv_sem.at[k],
                device_id=(fro if back else to, y),
                device_id_type=MESH,
            ).start()
            return carry

        lax.fori_loop(0, n - 1, one, 0)
        others = pl.ds(1, n - 1)
        return pltpu.make_async_remote_copy(
            src_ref=src.at[others],
            dst_ref=dst.at[others],
            send_sem=send_sem.at[k],
            recv_sem=recv_sem.at[k],
            device_id=(t, (y + 1) % n_branches),
            device_id_type=MESH,
        )

    a_bufs = ((a_send0, a_recv0), (a_send1, a_recv1))
    b_bufs = ((b_send0, b_recv0), (b_send1, b_recv1))
    g_bufs = ((g_send0, g_recv0), (g_send1, g_recv1))
    current = select[...]
    for step in range(STEPS):
        base = 3 * step
        a_send, a_recv = a_bufs[step]
        b_send, b_recv = b_bufs[step]
        g_send, g_recv = g_bufs[step]

        cur_o[...] = exact(current, pick_v[...], ROWS)

        def log_group(g, carry):
            if step == 0:
                fetch(g).wait()
            turned = pltpu.roll(cur_o[...], (WIDTH - GROUP * g) % WIDTH, 1)
            for i in range(GROUP):
                s = g * GROUP + i
                left = 1.0 - turned[:, i:i + 1] * tiles_v[s]
                left = left.reshape(CHAIN, WIDTH // CHAIN, WIDTH)
                part = left[0]
                for j in range(1, CHAIN):
                    part = part * left[j]
                logs_v[pl.ds(s, 1), :] = jnp.sum(jnp.log(part), axis=0, keepdims=True)
            return carry

        lax.fori_loop(0, groups, log_group, 0)
        logs = jnp.where(alive, logs_v[...], 0.0)
        packed = exact(route_v[...], logs, PLAIN)
        a_send[:, 0, :] = packed[0:n]
        a_send[:, 1, :] = packed[n:2 * n]
        if step == 0:
            pl.semaphore_wait(barrier, n - 1 + n_branches - 1)
        a_wait = send_all(a_send, a_recv, base, False)
        a_recv[0] = a_send[0]

        def term_group(g, carry):
            turned = pltpu.roll(cur_o[...], (WIDTH - GROUP * g) % WIDTH, 1)
            for i in range(GROUP):
                s = g * GROUP + i
                tile = tiles_v[s]
                terms_v[s] = tile / (1.0 - turned[:, i:i + 1] * tile)
            return carry

        lax.fori_loop(0, groups, term_group, 0)
        if step == 0:
            own_weights.wait()
        a_wait.wait_recv()

        if step == 0:
            tags = a_recv[:, 2, :]
            hold_v[...] = (
                tags == (iota((n, WIDTH), 1) % (WIDTH // 2)).astype(jnp.float32)
            ).astype(jnp.float32)
        hold = hold_v[...]
        both = jnp.concatenate([a_recv[:, 0, :], a_recv[:, 1, :]], axis=1)
        sums = exact(hold, both, ROWS)
        half = WIDTH // 2
        summed = sums[0:share, 0:WIDTH] + sums[half:half + share, WIDTH:]
        survival = weights_v[...] * jnp.exp(summed)
        gap = jnp.zeros((half - share, WIDTH), jnp.float32)
        none = jnp.zeros((half, WIDTH), jnp.float32)
        spread = jnp.concatenate(
            [
                jnp.concatenate([survival, gap, none], axis=0),
                jnp.concatenate([none, survival, gap], axis=0),
            ],
            axis=1,
        )
        replies = exact(hold, spread, PLAIN)
        b_send[:, 0, :] = replies[:, 0:WIDTH]
        b_send[:, 1, :] = replies[:, WIDTH:]
        b_wait = send_all(b_send, b_recv, base + 1, True)
        b_recv[0] = b_send[0]
        b_wait.wait_recv()
        got = jnp.concatenate([b_recv[:, 0, :], b_recv[:, 1, :]], axis=0)
        surv_v[...] = exact(route_v[...], got, ROWS)

        def grad_group(g, acc):
            for i in range(GROUP):
                s = g * GROUP + i
                col = jnp.sum(terms_v[s] * surv_v[pl.ds(s, 1), :], axis=1, keepdims=True)
                acc = jnp.where(iota((WIDTH, WIDTH), 1) == s, col, acc)
            return acc

        acc = lax.fori_loop(0, groups, grad_group, jnp.zeros((WIDTH, WIDTH), jnp.float32))
        parts = acc.T
        g_send[0:slots, :] = parts[0:slots]
        if step == 0:
            g_send[slots:slots + 8, :] = jnp.broadcast_to(row_of.astype(jnp.float32), (8, WIDTH))
        for d in (2, 1, 3):
            pltpu.make_async_remote_copy(
                src_ref=g_send,
                dst_ref=g_recv.at[y],
                send_sem=send_sem.at[base + 2],
                recv_sem=recv_sem.at[base + 2],
                device_id=(t, (y + d) % n_branches),
                device_id_type=MESH,
            ).start()
        g_recv[y] = g_send[...]
        g_wait = pltpu.make_async_remote_copy(
            src_ref=g_recv.at[pl.ds(0, n_branches - 1)],
            dst_ref=g_recv.at[pl.ds(0, n_branches - 1)],
            send_sem=send_sem.at[base + 2],
            recv_sem=recv_sem.at[base + 2],
            device_id=(t, (y + 1) % n_branches),
            device_id_type=MESH,
        )
        g_wait.wait_recv()
        if step == 0:
            for q in range(0, n_branches, 2):
                low = g_recv[q, slots:slots + 1, :]
                high = pltpu.roll(g_recv[q + 1, slots:slots + 8, :], WIDTH // 2, 1)[0:1]
                names = jnp.where(lane < slots, low, high)
                place_v[:, q * slots:(q + 2) * slots] = (
                    iota((WIDTH, WIDTH), 0).astype(jnp.float32) == names
                ).astype(jnp.float32)
        pieces = jnp.concatenate([g_recv[q, 0:slots, :] for q in range(n_branches)], axis=0)
        gradient = exact(place_v[...], pieces, PLAIN)
        rate = ascent_rate * gradient
        current = current + (select_cap - current) * rate / (1.0 + rate)
        a_wait.wait_send()
        b_wait.wait_send()
        g_wait.wait_send()
    grad_o[...] = gradient
    next_o[...] = current
    surv_o[...] = surv_v[0:slots, :]


def tiles_kernel(surv, cur, tiles, out):
    g = pl.program_id(0)
    turned = pltpu.roll(cur[...], (WIDTH - GROUP * g) % WIDTH, 1)
    for i in range(GROUP):
        picked = turned[:, i:i + 1]
        out[i] = surv[i:i + 1, :] * picked / (1.0 - picked * tiles[i])


def body(n, n_branches, select, tiles, row_block, col_block, counts, weights):
    slots = tiles.shape[0]
    test_rows = select.shape[0] // WIDTH
    branch_rows = weights.shape[0] // WIDTH
    share = branch_rows // n
    f32 = jnp.float32
    vmem = pl.BlockSpec(memory_space=pltpu.VMEM)
    hbm = pl.BlockSpec(memory_space=pl.ANY)
    square = jax.ShapeDtypeStruct((WIDTH, WIDTH), f32)
    message = lambda k: pltpu.VMEM((n, k, WIDTH), f32)
    grad_tests, next_select, surv, cur = pl.pallas_call(
        functools.partial(ascend_kernel, n, share, slots, n_branches),
        out_shape=(square, square, jax.ShapeDtypeStruct((slots, WIDTH), f32), square),
        in_specs=[vmem, vmem, vmem, vmem, hbm, hbm],
        out_specs=[vmem] * 4,
        scratch_shapes=[
            pltpu.VMEM(tiles.shape, f32),
            pltpu.VMEM(tiles.shape, f32),
            pltpu.VMEM((8, WIDTH), jnp.int32),
            pltpu.VMEM((WIDTH, WIDTH), f32),
            pltpu.VMEM((WIDTH, WIDTH), f32),
            pltpu.VMEM((WIDTH, WIDTH), f32),
            pltpu.VMEM((2 * n, WIDTH), f32),
            pltpu.VMEM((n, WIDTH), f32),
            pltpu.VMEM((WIDTH, n_branches * slots), f32),
            pltpu.VMEM((share, WIDTH), f32),
            message(3), message(3), message(2), message(2),
            message(2), message(2), message(2), message(2),
            pltpu.VMEM((slots + 8, WIDTH), f32),
            pltpu.VMEM((n_branches, slots + 8, WIDTH), f32),
            pltpu.VMEM((slots, WIDTH), f32),
            pltpu.VMEM((n_branches, slots, WIDTH), f32),
            pltpu.SemaphoreType.DMA((slots // GROUP,)),
            pltpu.SemaphoreType.DMA,
            pltpu.SemaphoreType.DMA((3 * STEPS,)),
            pltpu.SemaphoreType.DMA((3 * STEPS,)),
        ],
        compiler_params=pltpu.CompilerParams(
            collective_id=0, has_side_effects=True, vmem_limit_bytes=32 << 20
        ),
        name="ascend",
    )(
        select.reshape(test_rows, WIDTH),
        row_block.reshape(1, slots),
        col_block.reshape(1, slots),
        counts.reshape(1, 1),
        tiles,
        weights.reshape(branch_rows, WIDTH),
    )
    block = pl.BlockSpec((GROUP, WIDTH, WIDTH), lambda g: (g, 0, 0))
    tile_grads = pl.pallas_call(
        tiles_kernel,
        grid=(slots // GROUP,),
        out_shape=jax.ShapeDtypeStruct(tiles.shape, f32),
        in_specs=[
            pl.BlockSpec((GROUP, WIDTH), lambda g: (g, 0)),
            pl.BlockSpec((WIDTH, WIDTH), lambda g: (0, 0)),
            block,
        ],
        out_specs=block,
        name="tile_terms",
    )(surv, cur, tiles)
    return grad_tests.reshape(-1), tile_grads, next_select.reshape(-1)


def solution(mesh):
    n, n_branches = mesh.shape["tests"], mesh.shape["branches"]
    return jax.shard_map(
        functools.partial(body, n, n_branches),
        mesh=mesh,
        in_specs=(
            P("tests"),
            P(("tests", "branches"), None, None),
            P(("tests", "branches")),
            P(("tests", "branches")),
            P(("tests", "branches")),
            P("branches"),
        ),
        out_specs=(P("tests"), P(("tests", "branches"), None, None), P("tests")),
        check_vma=False,
    )
```

```python
import functools

import jax
import jax.numpy as jnp
from jax import lax
from jax.experimental import pallas as pl
from jax.experimental.pallas import tpu as pltpu
from jax.sharding import PartitionSpec as P

MESH = pl.DeviceIdType.MESH
STEPS = 2
WIDTH = 128
GROUP = 8
CHAIN = 16
Z, X, C = 8, 4, 2

ascent_rate = 0.0015
select_cap = 0.5

exact = functools.partial(
    lax.dot_general,
    precision=lax.Precision.HIGHEST,
    preferred_element_type=jnp.float32,
)
ROWS = (((0,), (0,)), ((), ()))
PLAIN = (((1,), (0,)), ((), ()))


def iota(shape, axis):
    return lax.broadcasted_iota(jnp.int32, shape, axis)


def zigzag(k, size):
    half = (k + 1) // 2
    return size // 2 + half * (1 - 2 * (k % 2))


def ascend_kernel(
    n, share, slots, n_branches,
    select_h, rows_h, cols_h, counts_h, tiles_h, weights_h,
    grad_o, next_o, tile_o,
    select, rows, cols, counts, cur_v, tiles_v, terms_v, meta_v, logs_v, surv_v, pick_v, route_v, hold_v, place_v, weights_v,
    a_send0, a_recv0, a_send1, a_recv1, b_send0, b_recv0, b_send1, b_recv1,
    g_send0, g_recv0, g_send1, g_recv1,
    tile_sem, local_sem, small_sem, send_sem, recv_sem,
):
    t = lax.axis_index("tests")
    y = lax.axis_index("branches")
    z, x, c = t // (X * C), (t // C) % X, t % C
    groups = slots // GROUP

    def fetch(g):
        part = pl.ds(pl.multiple_of(g * GROUP, GROUP), GROUP)
        return pltpu.make_async_copy(tiles_h.at[part], tiles_v.at[part], tile_sem.at[g])

    smalls = [
        pltpu.make_async_copy(src, dst, small_sem.at[i])
        for i, (src, dst) in enumerate(
            ((select_h, select), (rows_h, rows), (cols_h, cols), (counts_h, counts))
        )
    ]
    for copy in smalls:
        copy.start()
    for g in range(groups):
        fetch(g).start()
    own_weights = pltpu.make_async_copy(
        weights_h.at[pl.ds(pl.multiple_of(t * share, share), share)], weights_v, local_sem
    )
    own_weights.start()

    def ahead(i):
        dz, dx, dc = zigzag(i // (X * C), Z), zigzag((i // C) % X, X), 1 - i % C
        to = ((z + dz) % Z) * (X * C) + ((x + dx) % X) * C + (c + dc) % C
        back = ((z + Z - dz) % Z) * (X * C) + ((x + X - dx) % X) * C + (c + dc) % C
        return dz * (X * C) + dx * C + dc, to, back

    barrier = pltpu.get_barrier_semaphore()

    def greet(i, carry):
        _, to, _ = ahead(i)
        pl.semaphore_signal(barrier, inc=1, device_id=(to, y), device_id_type=MESH)
        return carry

    lax.fori_loop(0, n - 1, greet, 0)
    for d in range(1, n_branches):
        pl.semaphore_signal(
            barrier, inc=1, device_id=(t, (y + d) % n_branches), device_id_type=MESH
        )

    for copy in smalls:
        copy.wait()
    meta_v[...] = jnp.full_like(meta_v, -1)
    meta_v[0:1, 0:slots] = rows[...]
    meta_v[1:2, 0:slots] = cols[...]
    limit = counts[...]
    row_of, col_of = meta_v[0:1, :], meta_v[1:2, :]
    lane = iota((1, WIDTH), 1)
    live = lane < limit
    pick = (iota((WIDTH, WIDTH), 0) == row_of).astype(jnp.float32)
    pick_v[...] = pick
    owner, inside = col_of // share, col_of % share
    oz, ox, oc = owner // (X * C), (owner // C) % X, owner % C
    seat = ((oz + Z - z) % Z) * (X * C) + ((ox + X - x) % X) * C + (oc + C - c) % C
    seat = jnp.where(live, seat, n)
    takes = (iota((n, WIDTH), 0) == seat).astype(jnp.float32)
    earlier = (iota((WIDTH, WIDTH), 0) < iota((WIDTH, WIDTH), 1)).astype(jnp.float32)
    before = exact(takes, earlier, PLAIN)
    first = jnp.where(before < 0.5, takes, 0.0)
    second = takes - first
    route_v[0:n, :] = first
    route_v[n:2 * n, :] = second
    tag = (inside + 1).astype(jnp.float32)
    tag0 = jnp.sum(first * tag, axis=1, keepdims=True) - 1.0
    tag1 = jnp.sum(second * tag, axis=1, keepdims=True) - 1.0
    a_send0[:, 2, :] = jnp.where(iota((n, WIDTH), 1) < WIDTH // 2, tag0, tag1)

    logs_v[...] = jnp.zeros_like(logs_v)
    alive = iota((WIDTH, WIDTH), 0) < limit

    def send_all(src, dst, k, back):
        def one(i, carry):
            r, to, fro = ahead(i)
            pltpu.make_async_remote_copy(
                src_ref=src.at[r],
                dst_ref=dst.at[r],
                send_sem=send_sem.at[k],
                recv_sem=recv_sem.at[k],
                device_id=(fro if back else to, y),
                device_id_type=MESH,
            ).start()
            return carry

        lax.fori_loop(0, n - 1, one, 0)
        others = pl.ds(1, n - 1)
        return pltpu.make_async_remote_copy(
            src_ref=src.at[others],
            dst_ref=dst.at[others],
            send_sem=send_sem.at[k],
            recv_sem=recv_sem.at[k],
            device_id=(t, (y + 1) % n_branches),
            device_id_type=MESH,
        )

    a_bufs = ((a_send0, a_recv0), (a_send1, a_recv1))
    b_bufs = ((b_send0, b_recv0), (b_send1, b_recv1))
    g_bufs = ((g_send0, g_recv0), (g_send1, g_recv1))
    current = select[...]
    for step in range(STEPS):
        base = 3 * step
        last = step == STEPS - 1
        a_send, a_recv = a_bufs[step]
        b_send, b_recv = b_bufs[step]
        g_send, g_recv = g_bufs[step]

        cur_v[...] = exact(current, pick_v[...], ROWS)

        def log_group(g, carry):
            if step == 0:
                fetch(g).wait()
            turned = pltpu.roll(cur_v[...], (WIDTH - GROUP * g) % WIDTH, 1)
            for i in range(GROUP):
                s = g * GROUP + i
                left = 1.0 - turned[:, i:i + 1] * tiles_v[s]
                left = left.reshape(CHAIN, WIDTH // CHAIN, WIDTH)
                part = left[0]
                for j in range(1, CHAIN):
                    part = part * left[j]
                logs_v[pl.ds(s, 1), :] = jnp.sum(jnp.log(part), axis=0, keepdims=True)
            return carry

        lax.fori_loop(0, groups, log_group, 0)
        logs = jnp.where(alive, logs_v[...], 0.0)
        packed = exact(route_v[...], logs, PLAIN)
        a_send[:, 0, :] = packed[0:n]
        a_send[:, 1, :] = packed[n:2 * n]
        if step == 0:
            pl.semaphore_wait(barrier, n - 1 + n_branches - 1)
        a_wait = send_all(a_send, a_recv, base, False)
        a_recv[0] = a_send[0]

        def term_group(g, carry):
            turned = pltpu.roll(cur_v[...], (WIDTH - GROUP * g) % WIDTH, 1)
            for i in range(GROUP):
                s = g * GROUP + i
                tile = tiles_v[s]
                picked = turned[:, i:i + 1]
                inverse = 1.0 / (1.0 - picked * tile)
                terms_v[s] = tile * inverse
                if last:
                    tile_o[s] = picked * inverse
            return carry

        lax.fori_loop(0, groups, term_group, 0)
        if step == 0:
            own_weights.wait()
        a_wait.wait_recv()

        if step == 0:
            tags = a_recv[:, 2, :]
            hold_v[...] = (
                tags == (iota((n, WIDTH), 1) % (WIDTH // 2)).astype(jnp.float32)
            ).astype(jnp.float32)
        hold = hold_v[...]
        both = jnp.concatenate([a_recv[:, 0, :], a_recv[:, 1, :]], axis=1)
        sums = exact(hold, both, ROWS)
        half = WIDTH // 2
        summed = sums[0:share, 0:WIDTH] + sums[half:half + share, WIDTH:]
        survival = weights_v[...] * jnp.exp(summed)
        gap = jnp.zeros((half - share, WIDTH), jnp.float32)
        none = jnp.zeros((half, WIDTH), jnp.float32)
        spread = jnp.concatenate(
            [
                jnp.concatenate([survival, gap, none], axis=0),
                jnp.concatenate([none, survival, gap], axis=0),
            ],
            axis=1,
        )
        replies = exact(hold, spread, PLAIN)
        b_send[:, 0, :] = replies[:, 0:WIDTH]
        b_send[:, 1, :] = replies[:, WIDTH:]
        b_wait = send_all(b_send, b_recv, base + 1, True)
        b_recv[0] = b_send[0]
        b_wait.wait_recv()
        got = jnp.concatenate([b_recv[:, 0, :], b_recv[:, 1, :]], axis=0)
        surv_v[...] = jnp.where(alive, exact(route_v[...], got, ROWS), 0.0)

        def grad_group(g, acc):
            for i in range(GROUP):
                s = g * GROUP + i
                col = jnp.sum(terms_v[s] * surv_v[pl.ds(s, 1), :], axis=1, keepdims=True)
                acc = jnp.where(iota((WIDTH, WIDTH), 1) == s, col, acc)
            return acc

        acc = lax.fori_loop(0, groups, grad_group, jnp.zeros((WIDTH, WIDTH), jnp.float32))
        parts = acc.T
        g_send[0:slots, :] = parts[0:slots]
        if step == 0:
            g_send[slots:slots + 8, :] = jnp.broadcast_to(row_of.astype(jnp.float32), (8, WIDTH))
        for d in (2, 1, 3):
            pltpu.make_async_remote_copy(
                src_ref=g_send,
                dst_ref=g_recv.at[y],
                send_sem=send_sem.at[base + 2],
                recv_sem=recv_sem.at[base + 2],
                device_id=(t, (y + d) % n_branches),
                device_id_type=MESH,
            ).start()
        g_recv[y] = g_send[...]
        g_wait = pltpu.make_async_remote_copy(
            src_ref=g_recv.at[pl.ds(0, n_branches - 1)],
            dst_ref=g_recv.at[pl.ds(0, n_branches - 1)],
            send_sem=send_sem.at[base + 2],
            recv_sem=recv_sem.at[base + 2],
            device_id=(t, (y + 1) % n_branches),
            device_id_type=MESH,
        )
        if last:

            def tile_group(g, carry):
                for i in range(GROUP):
                    s = g * GROUP + i
                    tile_o[s] = tile_o[s] * surv_v[pl.ds(s, 1), :]
                return carry

            lax.fori_loop(0, groups, tile_group, 0)
        g_wait.wait_recv()
        if step == 0:
            for q in range(0, n_branches, 2):
                low = g_recv[q, slots:slots + 1, :]
                high = pltpu.roll(g_recv[q + 1, slots:slots + 8, :], WIDTH // 2, 1)[0:1]
                names = jnp.where(lane < slots, low, high)
                place_v[:, q * slots:(q + 2) * slots] = (
                    iota((WIDTH, WIDTH), 0).astype(jnp.float32) == names
                ).astype(jnp.float32)
        pieces = jnp.concatenate([g_recv[q, 0:slots, :] for q in range(n_branches)], axis=0)
        gradient = exact(place_v[...], pieces, PLAIN)
        rate = ascent_rate * gradient
        current = current + (select_cap - current) * rate / (1.0 + rate)
        a_wait.wait_send()
        b_wait.wait_send()
        g_wait.wait_send()
    grad_o[...] = gradient
    next_o[...] = current


def store_kernel(count, *refs):
    copies = [
        pltpu.make_async_copy(refs[i], refs[count + i], refs[2 * count].at[i])
        for i in range(count)
    ]
    for copy in copies:
        copy.start()
    for copy in copies:
        copy.wait()


def body(n, n_branches, select, tiles, row_block, col_block, counts, weights):
    slots = tiles.shape[0]
    test_rows = select.shape[0] // WIDTH
    branch_rows = weights.shape[0] // WIDTH
    share = branch_rows // n
    f32 = jnp.float32
    vmem = pl.BlockSpec(memory_space=pltpu.VMEM)
    hbm = pl.BlockSpec(memory_space=pltpu.HBM)
    square = jax.ShapeDtypeStruct((WIDTH, WIDTH), f32)
    shapes = (square, square, jax.ShapeDtypeStruct(tiles.shape, f32))
    held = tuple(pltpu.VMEM(a.shape, f32) for a in shapes)
    stay = lambda a: pltpu.with_memory_space_constraint(a, pltpu.HBM)
    message = lambda k: pltpu.VMEM((n, k, WIDTH), f32)
    results = pl.pallas_call(
        functools.partial(ascend_kernel, n, share, slots, n_branches),
        out_shape=held,
        in_specs=[hbm] * 6,
        out_specs=[vmem] * 3,
        scratch_shapes=[
            pltpu.VMEM((test_rows, WIDTH), f32),
            pltpu.VMEM((1, slots), jnp.int32),
            pltpu.VMEM((1, slots), jnp.int32),
            pltpu.VMEM((1, 1), jnp.int32),
            pltpu.VMEM((WIDTH, WIDTH), f32),
            pltpu.VMEM(tiles.shape, f32),
            pltpu.VMEM(tiles.shape, f32),
            pltpu.VMEM((8, WIDTH), jnp.int32),
            pltpu.VMEM((WIDTH, WIDTH), f32),
            pltpu.VMEM((WIDTH, WIDTH), f32),
            pltpu.VMEM((WIDTH, WIDTH), f32),
            pltpu.VMEM((2 * n, WIDTH), f32),
            pltpu.VMEM((n, WIDTH), f32),
            pltpu.VMEM((WIDTH, n_branches * slots), f32),
            pltpu.VMEM((share, WIDTH), f32),
            message(3), message(3), message(2), message(2),
            message(2), message(2), message(2), message(2),
            pltpu.VMEM((slots + 8, WIDTH), f32),
            pltpu.VMEM((n_branches, slots + 8, WIDTH), f32),
            pltpu.VMEM((slots, WIDTH), f32),
            pltpu.VMEM((n_branches, slots, WIDTH), f32),
            pltpu.SemaphoreType.DMA((slots // GROUP,)),
            pltpu.SemaphoreType.DMA,
            pltpu.SemaphoreType.DMA((4,)),
            pltpu.SemaphoreType.DMA((3 * STEPS,)),
            pltpu.SemaphoreType.DMA((3 * STEPS,)),
        ],
        compiler_params=pltpu.CompilerParams(
            collective_id=0, has_side_effects=True, vmem_limit_bytes=59 << 20
        ),
        name="ascend",
    )(
        select.reshape(test_rows, WIDTH),
        row_block.reshape(1, slots),
        col_block.reshape(1, slots),
        counts.reshape(1, 1),
        tiles,
        weights.reshape(branch_rows, WIDTH),
    )
    grad_tests, next_select, tile_grads = pl.pallas_call(
        functools.partial(store_kernel, len(shapes)),
        out_shape=shapes,
        in_specs=[vmem] * len(shapes),
        out_specs=[hbm] * len(shapes),
        scratch_shapes=[pltpu.SemaphoreType.DMA((len(shapes),))],
        compiler_params=pltpu.CompilerParams(vmem_limit_bytes=1 << 20),
        name="store",
    )(*results)
    return grad_tests.reshape(-1), tile_grads, next_select.reshape(-1)


def solution(mesh):
    n, n_branches = mesh.shape["tests"], mesh.shape["branches"]
    return jax.shard_map(
        functools.partial(body, n, n_branches),
        mesh=mesh,
        in_specs=(
            P("tests"),
            P(("tests", "branches"), None, None),
            P(("tests", "branches")),
            P(("tests", "branches")),
            P(("tests", "branches")),
            P("branches"),
        ),
        out_specs=(P("tests"), P(("tests", "branches"), None, None), P("tests")),
        check_vma=False,
    )
```

```python
import functools

import jax
import jax.numpy as jnp
from jax import lax
from jax.experimental import pallas as pl
from jax.experimental.pallas import tpu as pltpu
from jax.sharding import PartitionSpec as P

MESH = pl.DeviceIdType.MESH
STEPS = 2
HALVES = 2
PIECES = 8
WIDTH = 128
GROUP = 8
CHAIN = 16
Z, X, C = 8, 4, 2

ascent_rate = 0.0015
select_cap = 0.5

ROWS = (((0,), (0,)), ((), ()))
PLAIN = (((1,), (0,)), ((), ()))


def thirds(x):
    high = x.astype(jnp.bfloat16)
    rest = x - high.astype(jnp.float32)
    middle = rest.astype(jnp.bfloat16)
    low = (rest - middle.astype(jnp.float32)).astype(jnp.bfloat16)
    return low, middle, high


def dot(a, b, dims):
    return lax.dot_general(a, b, dims, preferred_element_type=jnp.float32)


def select_by(mask, x, dims):
    low, middle, high = (dot(mask.astype(jnp.bfloat16), part, dims) for part in thirds(x))
    return low + middle + high


def iota(shape, axis):
    return lax.broadcasted_iota(jnp.int32, shape, axis)


def zigzag(k, size):
    half = (k + 1) // 2
    return size // 2 + half * (1 - 2 * (k % 2))


def ascend_kernel(
    n, share, slots, n_branches,
    select_h, rows_h, cols_h, counts_h, tiles_h, weights_h,
    grad_o, next_o, tile_o,
    select, rows, cols, counts, cur_v, tiles_v, terms_v, meta_v, logs_v, surv_v, pick_v, route_v, hold_v, place_v, weights_v,
    a_send0, a_recv0, a_send1, a_recv1, b_send0, b_recv0, b_send1, b_recv1,
    g_send0, g_recv0, g_send1, g_recv1,
    tile_sem, local_sem, small_sem, send_sem, recv_sem,
):
    t = lax.axis_index("tests")
    y = lax.axis_index("branches")
    z, x, c = t // (X * C), (t // C) % X, t % C
    groups = slots // GROUP

    def fetch(g):
        part = pl.ds(pl.multiple_of(g * GROUP, GROUP), GROUP)
        return pltpu.make_async_copy(tiles_h.at[part], tiles_v.at[part], tile_sem.at[g])

    smalls = [
        pltpu.make_async_copy(src, dst, small_sem.at[i])
        for i, (src, dst) in enumerate(
            ((select_h, select), (rows_h, rows), (cols_h, cols), (counts_h, counts))
        )
    ]
    for copy in smalls:
        copy.start()
    def ahead(i):
        dz, dx, dc = zigzag(i // (X * C), Z), zigzag((i // C) % X, X), 1 - i % C
        to = ((z + dz) % Z) * (X * C) + ((x + dx) % X) * C + (c + dc) % C
        back = ((z + Z - dz) % Z) * (X * C) + ((x + X - dx) % X) * C + (c + dc) % C
        return dz * (X * C) + dx * C + dc, to, back

    barrier = pltpu.get_barrier_semaphore()

    def greet(i, carry):
        _, to, _ = ahead(i)
        pl.semaphore_signal(barrier, inc=1, device_id=(to, y), device_id_type=MESH)
        return carry

    lax.fori_loop(0, n - 1, greet, 0)
    for d in range(1, n_branches):
        pl.semaphore_signal(
            barrier, inc=1, device_id=(t, (y + d) % n_branches), device_id_type=MESH
        )

    for g in range(groups):
        fetch(g).start()
    own_weights = pltpu.make_async_copy(
        weights_h.at[pl.ds(pl.multiple_of(t * share, share), share)], weights_v, local_sem
    )
    own_weights.start()

    for copy in smalls:
        copy.wait()
    meta_v[...] = jnp.full_like(meta_v, -1)
    meta_v[0:1, 0:slots] = rows[...]
    meta_v[1:2, 0:slots] = cols[...]
    limit = counts[...]
    row_of, col_of = meta_v[0:1, :], meta_v[1:2, :]
    lane = iota((1, WIDTH), 1)
    live = lane < limit
    pick = (iota((WIDTH, WIDTH), 0) == row_of).astype(jnp.float32)
    pick_v[...] = pick
    owner, inside = col_of // share, col_of % share
    oz, ox, oc = owner // (X * C), (owner // C) % X, owner % C
    seat = ((oz + Z - z) % Z) * (X * C) + ((ox + X - x) % X) * C + (oc + C - c) % C
    seat = jnp.where(live, seat, n)
    takes = (iota((n, WIDTH), 0) == seat).astype(jnp.float32)
    earlier = (iota((WIDTH, WIDTH), 0) < iota((WIDTH, WIDTH), 1)).astype(jnp.float32)
    before = dot(takes.astype(jnp.bfloat16), earlier.astype(jnp.bfloat16), PLAIN)
    first = jnp.where(before < 0.5, takes, 0.0)
    second = takes - first
    route_v[0:n, :] = first
    route_v[n:2 * n, :] = second
    tag = (inside + 1).astype(jnp.float32)
    tag0 = jnp.sum(first * tag, axis=1, keepdims=True) - 1.0
    tag1 = jnp.sum(second * tag, axis=1, keepdims=True) - 1.0
    a_send0[:, 2, :] = jnp.where(iota((n, WIDTH), 1) < WIDTH // 2, tag0, tag1)

    g_send0[slots:slots + 8, :] = jnp.broadcast_to(row_of.astype(jnp.float32), (8, WIDTH))

    logs_v[...] = jnp.zeros_like(logs_v)
    alive = iota((WIDTH, WIDTH), 0) < limit

    def send_all(src, dst, k, back):
        def one(i, carry):
            r, to, fro = ahead(i)
            pltpu.make_async_remote_copy(
                src_ref=src.at[r],
                dst_ref=dst.at[r],
                send_sem=send_sem.at[k],
                recv_sem=recv_sem.at[k],
                device_id=(fro if back else to, y),
                device_id_type=MESH,
            ).start()
            return carry

        lax.fori_loop(0, n - 1, one, 0)
        others = pl.ds(1, n - 1)
        return pltpu.make_async_remote_copy(
            src_ref=src.at[others],
            dst_ref=dst.at[others],
            send_sem=send_sem.at[k],
            recv_sem=recv_sem.at[k],
            device_id=(t, (y + 1) % n_branches),
            device_id_type=MESH,
        )

    a_bufs = ((a_send0, a_recv0), (a_send1, a_recv1))
    b_bufs = ((b_send0, b_recv0), (b_send1, b_recv1))
    g_bufs = ((g_send0, g_recv0), (g_send1, g_recv1))
    current = select[...]
    for step in range(STEPS):
        base = 3 * step
        last = step == STEPS - 1
        a_send, a_recv = a_bufs[step]
        b_send, b_recv = b_bufs[step]
        g_send, g_recv = g_bufs[step]

        picks = pick_v[...].astype(jnp.bfloat16)
        low, middle, high = (dot(part, picks, ROWS) for part in thirds(current))
        cur_v[...] = low + middle + high

        def log_group(g, carry):
            if step == 0:
                fetch(g).wait()
            turned = pltpu.roll(cur_v[...], (WIDTH - GROUP * g) % WIDTH, 1)
            for i in range(GROUP):
                s = g * GROUP + i
                left = 1.0 - turned[:, i:i + 1] * tiles_v[s]
                left = left.reshape(CHAIN, WIDTH // CHAIN, WIDTH)
                part = left[0]
                for j in range(1, CHAIN):
                    part = part * left[j]
                logs_v[pl.ds(s, 1), :] = jnp.sum(jnp.log(part), axis=0, keepdims=True)
            return carry

        lax.fori_loop(0, groups, log_group, 0)
        logs = jnp.where(alive, logs_v[...], 0.0)
        packed = select_by(route_v[...], logs, PLAIN)
        a_send[:, 0, :] = packed[0:n]
        a_send[:, 1, :] = packed[n:2 * n]
        if step == 0:
            pl.semaphore_wait(barrier, n - 1 + n_branches - 1)
        a_wait = send_all(a_send, a_recv, base, False)
        a_recv[0] = a_send[0]

        def send_rows(start, count):
            part = pl.ds(start, count)
            for d in (2, 1, 3):
                pltpu.make_async_remote_copy(
                    src_ref=g_send.at[part],
                    dst_ref=g_recv.at[y, part],
                    send_sem=send_sem.at[base + 2],
                    recv_sem=recv_sem.at[base + 2],
                    device_id=(t, (y + d) % n_branches),
                    device_id_type=MESH,
                ).start()

        if step == 0:
            send_rows(slots, 8)

        def term_group(g, carry):
            turned = pltpu.roll(cur_v[...], (WIDTH - GROUP * g) % WIDTH, 1)
            for i in range(GROUP):
                s = g * GROUP + i
                tile = tiles_v[s]
                picked = turned[:, i:i + 1]
                inverse = 1.0 / (1.0 - picked * tile)
                terms_v[s] = tile * inverse
                if last:
                    tile_o[s] = picked * inverse
            return carry

        lax.fori_loop(0, groups, term_group, 0)
        if step == 0:
            own_weights.wait()
        a_wait.wait_recv()

        if step == 0:
            tags = a_recv[:, 2, :]
            hold_v[...] = (
                tags == (iota((n, WIDTH), 1) % (WIDTH // 2)).astype(jnp.float32)
            ).astype(jnp.float32)
        hold = hold_v[...]
        both = jnp.concatenate([a_recv[:, 0, :], a_recv[:, 1, :]], axis=1)
        sums = select_by(hold, both, ROWS)
        half = WIDTH // 2
        summed = sums[0:share, 0:WIDTH] + sums[half:half + share, WIDTH:]
        survival = weights_v[...] * jnp.exp(summed)
        gap = jnp.zeros((half - share, WIDTH), jnp.float32)
        none = jnp.zeros((half, WIDTH), jnp.float32)
        spread = jnp.concatenate(
            [
                jnp.concatenate([survival, gap, none], axis=0),
                jnp.concatenate([none, survival, gap], axis=0),
            ],
            axis=1,
        )
        replies = select_by(hold, spread, PLAIN)
        b_send[:, 0, :] = replies[:, 0:WIDTH]
        b_send[:, 1, :] = replies[:, WIDTH:]
        b_wait = send_all(b_send, b_recv, base + 1, True)
        b_recv[0] = b_send[0]
        b_wait.wait_recv()
        got = jnp.concatenate([b_recv[:, 0, :], b_recv[:, 1, :]], axis=0)
        surv_v[...] = jnp.where(alive, select_by(route_v[...], got, ROWS), 0.0)

        def grad_group(g, acc):
            for i in range(GROUP):
                s = g * GROUP + i
                col = jnp.sum(terms_v[s] * surv_v[pl.ds(s, 1), :], axis=1, keepdims=True)
                acc = jnp.where(iota((WIDTH, WIDTH), 1) == s, col, acc)
            return acc

        for h in range(HALVES):
            acc = lax.fori_loop(
                h * groups // HALVES,
                (h + 1) * groups // HALVES,
                grad_group,
                jnp.zeros((WIDTH, WIDTH), jnp.float32),
            )
            start, count = h * slots // HALVES, slots // HALVES
            g_send[start:start + count, :] = acc.T[start:start + count]
            send_rows(start, count)
        g_recv[y] = g_send[...]
        g_wait = pltpu.make_async_remote_copy(
            src_ref=g_recv.at[pl.ds(0, n_branches - 1)],
            dst_ref=g_recv.at[pl.ds(0, n_branches - 1)],
            send_sem=send_sem.at[base + 2],
            recv_sem=recv_sem.at[base + 2],
            device_id=(t, (y + 1) % n_branches),
            device_id_type=MESH,
        )
        if last:

            def tile_group(g, carry):
                for i in range(GROUP):
                    s = g * GROUP + i
                    tile_o[s] = tile_o[s] * surv_v[pl.ds(s, 1), :]
                return carry

            lax.fori_loop(0, groups, tile_group, 0)
        g_wait.wait_recv()
        if step == 0:
            for q in range(0, n_branches, 2):
                low = g_recv[q, slots:slots + 1, :]
                high = pltpu.roll(g_recv[q + 1, slots:slots + 8, :], WIDTH // 2, 1)[0:1]
                names = jnp.where(lane < slots, low, high)
                place_v[:, q * slots:(q + 2) * slots] = (
                    iota((WIDTH, WIDTH), 0).astype(jnp.float32) == names
                ).astype(jnp.float32)
        pieces = jnp.concatenate([g_recv[q, 0:slots, :] for q in range(n_branches)], axis=0)
        gradient = select_by(place_v[...], pieces, PLAIN)
        rate = ascent_rate * gradient
        current = current + (select_cap - current) * rate / (1.0 + rate)
        a_wait.wait_send()
        b_wait.wait_send()
        g_wait.wait_send()
    grad_o[...] = gradient
    next_o[...] = current


def store_kernel(count, *refs):
    sems = refs[2 * count]
    copies = []
    for i in reversed(range(count)):
        src, dst = refs[i], refs[count + i]
        rows = src.shape[0]
        size = rows // PIECES if len(src.shape) == 3 else rows
        for start in range(0, rows, size):
            part = pl.ds(start, size)
            copies.append(
                pltpu.make_async_copy(src.at[part], dst.at[part], sems.at[len(copies)])
            )
    for copy in copies:
        copy.start()
    for copy in copies:
        copy.wait()


def body(n, n_branches, select, tiles, row_block, col_block, counts, weights):
    slots = tiles.shape[0]
    test_rows = select.shape[0] // WIDTH
    branch_rows = weights.shape[0] // WIDTH
    share = branch_rows // n
    f32 = jnp.float32
    vmem = pl.BlockSpec(memory_space=pltpu.VMEM)
    hbm = pl.BlockSpec(memory_space=pltpu.HBM)
    square = jax.ShapeDtypeStruct((WIDTH, WIDTH), f32)
    shapes = (square, square, jax.ShapeDtypeStruct(tiles.shape, f32))
    held = tuple(pltpu.VMEM(a.shape, f32) for a in shapes)
    stay = lambda a: pltpu.with_memory_space_constraint(a, pltpu.HBM)
    message = lambda k: pltpu.VMEM((n, k, WIDTH), f32)
    results = pl.pallas_call(
        functools.partial(ascend_kernel, n, share, slots, n_branches),
        out_shape=held,
        in_specs=[hbm] * 6,
        out_specs=[vmem] * 3,
        scratch_shapes=[
            pltpu.VMEM((test_rows, WIDTH), f32),
            pltpu.VMEM((1, slots), jnp.int32),
            pltpu.VMEM((1, slots), jnp.int32),
            pltpu.VMEM((1, 1), jnp.int32),
            pltpu.VMEM((WIDTH, WIDTH), f32),
            pltpu.VMEM(tiles.shape, f32),
            pltpu.VMEM(tiles.shape, f32),
            pltpu.VMEM((8, WIDTH), jnp.int32),
            pltpu.VMEM((WIDTH, WIDTH), f32),
            pltpu.VMEM((WIDTH, WIDTH), f32),
            pltpu.VMEM((WIDTH, WIDTH), f32),
            pltpu.VMEM((2 * n, WIDTH), f32),
            pltpu.VMEM((n, WIDTH), f32),
            pltpu.VMEM((WIDTH, n_branches * slots), f32),
            pltpu.VMEM((share, WIDTH), f32),
            message(3), message(3), message(2), message(2),
            message(2), message(2), message(2), message(2),
            pltpu.VMEM((slots + 8, WIDTH), f32),
            pltpu.VMEM((n_branches, slots + 8, WIDTH), f32),
            pltpu.VMEM((slots, WIDTH), f32),
            pltpu.VMEM((n_branches, slots, WIDTH), f32),
            pltpu.SemaphoreType.DMA((slots // GROUP,)),
            pltpu.SemaphoreType.DMA,
            pltpu.SemaphoreType.DMA((4,)),
            pltpu.SemaphoreType.DMA((3 * STEPS,)),
            pltpu.SemaphoreType.DMA((3 * STEPS,)),
        ],
        compiler_params=pltpu.CompilerParams(
            collective_id=0, has_side_effects=True, vmem_limit_bytes=59 << 20
        ),
        name="ascend",
    )(
        select.reshape(test_rows, WIDTH),
        row_block.reshape(1, slots),
        col_block.reshape(1, slots),
        counts.reshape(1, 1),
        tiles,
        weights.reshape(branch_rows, WIDTH),
    )
    grad_tests, next_select, tile_grads = pl.pallas_call(
        functools.partial(store_kernel, len(shapes)),
        out_shape=shapes,
        in_specs=[vmem] * len(shapes),
        out_specs=[hbm] * len(shapes),
        scratch_shapes=[pltpu.SemaphoreType.DMA((len(shapes) - 1 + PIECES,))],
        compiler_params=pltpu.CompilerParams(vmem_limit_bytes=1 << 20),
        name="store",
    )(*results)
    return grad_tests.reshape(-1), tile_grads, next_select.reshape(-1)


def solution(mesh):
    n, n_branches = mesh.shape["tests"], mesh.shape["branches"]
    return jax.shard_map(
        functools.partial(body, n, n_branches),
        mesh=mesh,
        in_specs=(
            P("tests"),
            P(("tests", "branches"), None, None),
            P(("tests", "branches")),
            P(("tests", "branches")),
            P(("tests", "branches")),
            P("branches"),
        ),
        out_specs=(P("tests"), P(("tests", "branches"), None, None), P("tests")),
        check_vma=False,
    )
```
